32 devices in a mesh: space: 16 (over z, y, x), chan: 2 (over core).
Axes of the slice: x: 2, y: 2, z: 4, core: 2. Of those that a mesh axis runs over, the one named last changes fastest.
Arguments:
- source: bfloat16 [512, 48, 128], P('chan', 'space'), may hold values from -6 to 6
- kernel: bfloat16 [7, 7, 512, 512], P(None, None, 'chan'), may hold values from -0.0390625 to 0.0390625
Outputs:
- image: bfloat16 [512, 48, 128], P('chan', 'space')
The draws below stay inside these ranges and needn't reach their ends.
All inputs are finite; a program needn't handle non-finite values.
Results may differ from the reference program's by a relative error of at most 0.001.
Values may be sent and summed in bfloat16 or wider, within the bound.
No kernel may reach another device: no remote copies, remote signals or barrier semaphores. Data moves between devices by JAX's collectives and lax.ppermute only.
A program may use at most 64 MiB of HBM per device.

```python
import jax
import jax.numpy as jnp
from jax import lax

CH = 512
OFF = 7
NY = 128
NX = 48


def shard_levels(own_key, shape, pieces, low, high):
    gain = 1.0
    for dim, shards_of in pieces:
        heights = jax.random.uniform(jax.random.fold_in(jax.random.fold_in(own_key, 6), dim), (shards_of,), jnp.float32, low / len(pieces), high / len(pieces))
        gain = gain * jnp.repeat(jnp.exp(heights), shape[dim] // shards_of).reshape((-1,) + (1,) * (len(shape) - 1 - dim))
    return gain


def bell_draw(own_key, shape, deviation, most, split=(), kind=jnp.bfloat16):
    entries = jax.random.normal(own_key, shape, jnp.float32) * deviation
    if len(split) > 0:
        entries = shard_levels(own_key, shape, split, -0.22, 0.18) * entries
    return jnp.clip(entries, min=-most, max=most).astype(kind)


def setup_inputs(seed: int = 0) -> dict:
    streams_of = jax.random.split(jax.random.key(seed), 3)
    return {
        "source": bell_draw(streams_of[0], (CH, NX, NY), 1.0, 6.0, ((0, 2), (1, 16))),
        "kernel": bell_draw(streams_of[1], (OFF, OFF, CH, CH), (OFF * OFF * CH) ** -0.5, 0.0390625, ((2, 2),)),
    }


def reference(source, kernel):
    reach = (OFF - 1) // 2
    values = source.astype(jnp.float32)
    padded = jnp.pad(values, ((0, 0), (reach, reach), (reach, reach)))
    total = jnp.zeros(values.shape, jnp.float32)
    for row_shift in range(OFF):
        stacked = jnp.stack([padded[:, row_shift:row_shift + NX, col_shift:col_shift + NY] for col_shift in range(OFF)])
        blocks = kernel[row_shift].astype(jnp.float32)
        total = total + jnp.einsum("boc,bcxy->oxy", blocks, stacked, precision=lax.Precision.HIGHEST)
    return (values - total).astype(jnp.bfloat16)
```

```python
import functools

import jax
import jax.numpy as jnp
from jax import lax
from jax.experimental import pallas as pl
from jax.experimental.pallas import tpu as pltpu
from jax.sharding import PartitionSpec as P

OFF = 7
REACH = (OFF - 1) // 2
MXU = 256
LANES = 128
EDGE = 8
UNITS = 2


def padded_2(array, sides, width):
    for axis, dim in sides:
        devices, length = (lax.axis_size(axis), array.shape[dim])
        up = [(i, (i + 1) % devices) for i in range(devices - 1)]
        down = [(j, i) for i, j in up]
        last = lax.slice_in_dim(array, length - width, length, axis=dim)
        initial = lax.slice_in_dim(array, 0, width, axis=dim)
        before = lax.ppermute(last, axis, up)
        after = lax.ppermute(initial, axis, down)
        array = jnp.concatenate([before, array, after], axis=dim)
    return array


def correlate(kernel, padded, height):
    width_cols = padded.shape[2]
    widened = jnp.pad(padded, ((0, 0), (0, 0), (REACH, REACH)))
    total = jnp.zeros((kernel.shape[2], height, width_cols), jnp.float32)
    for row_shift in range(OFF):
        window = widened[:, row_shift : row_shift + height, :]
        stacked = jnp.stack(
            [window[:, :, col_shift : col_shift + width_cols] for col_shift in range(OFF)]
        )
        weights = kernel[row_shift]
        total = total + jnp.einsum(
            "boc,bcxy->oxy", weights, stacked, preferred_element_type=jnp.float32
        )
    return total


def general(source, kernel):
    height = source.shape[1]
    gathered = lax.all_gather(source, "chan", axis=0, tiled=True)
    rimmed = padded_2(gathered, (("space", 1),), REACH)
    coupled = correlate(kernel, rimmed, height)
    return (source.astype(jnp.float32) - coupled).astype(jnp.bfloat16)


def spread(block, row_of, pad, shifted):
    rows = block.shape[0]
    for q in range(rows):
        turned = block[row_of(q)].astype(jnp.float32).T
        for part in range(MXU // LANES):
            lanes = slice(part * LANES, (part + 1) * LANES)
            pad[q, part, pl.ds(EDGE, LANES), :] = turned[:, lanes]
            for b in range(OFF):
                view = pad[q, part, pl.ds(EDGE + b - REACH, LANES), :]
                shifted[b, q, :, lanes] = view.astype(jnp.bfloat16)


def clear_edges(pad):
    rows, parts = pad.shape[:2]
    blank = jnp.zeros((EDGE, LANES), jnp.float32)
    for q in range(rows):
        for part in range(parts):
            pad[q, part, pl.ds(0, EDGE), :] = blank
            pad[q, part, pl.ds(EDGE + LANES, EDGE), :] = blank


def multiply(tiles, weights, shifted, sums):
    rows = len(sums) // UNITS
    load, stage = [0] * UNITS, [0] * UNITS
    for n, a, half, b, pairs in tiles:
        unit = load.index(min(load))
        load[unit] += max(len(pairs), 2)
        slot = stage[unit]
        stage[unit] ^= 1
        lanes = pl.ds(pl.multiple_of(half * MXU, MXU), MXU)
        pltpu.matmul_push_rhs(
            weights[a, b, :, lanes], staging_register=slot, mxu_index=unit, transpose=True
        )
        for order, (q, i) in enumerate(pairs):
            pltpu.matmul_acc_lhs(
                sums[unit * rows + i],
                shifted[n, b, q],
                load_staged_rhs=slot if order == 0 else None,
            )


def collect(sums, i):
    rows = len(sums) // UNITS
    value = pltpu.matmul_pop(sums[i])
    for unit in range(1, UNITS):
        value = value + pltpu.matmul_pop(sums[unit * rows + i])
    return value


def with_sums(rows, body):
    refs = [
        pltpu.ACC(unit)((LANES, MXU), jnp.float32) for unit in range(UNITS) for _ in range(rows)
    ]
    pl.run_scoped(lambda *sums: body(sums), *refs)


def own_kernel(place, *refs):
    *blocks, weights, total, pad, shifted = refs
    rows = blocks[0].shape[0]

    def body(sums):
        clear_edges(pad)
        tiles = []
        for n, block in enumerate(blocks):
            spread(block, lambda q: q, pad, shifted.at[n])
            half = place[n]
            for b in range(OFF):
                for a in range(OFF):
                    pairs = [(q, q - a + REACH) for q in range(rows)]
                    pairs = [(q, i) for q, i in pairs if 0 <= i < rows]
                    if pairs:
                        tiles.append((n, a, half, b, pairs))
        multiply(tiles, weights, shifted, sums)
        for i in range(rows):
            total[i] = collect(sums, i)

    with_sums(rows, body)


def halo_terms(place, blocks, halves, weights, pad, shifted, sums):
    rows = blocks[0].shape[0]
    flip = place[2]
    clear_edges(pad)
    tiles = []
    for n, block in enumerate(blocks):
        spread(block, lambda q: q + flip * (rows - 1 - 2 * q), pad, shifted.at[n])
        for b in range(OFF):
            for t in range(rows):
                a = t + flip * (OFF - 1 - 2 * t)
                tiles.append((n, a, halves[n], b, [(m + t, m) for m in range(rows - t)]))
    multiply(tiles, weights, shifted, sums)


def halo_kernel(halves, place, *refs):
    *blocks, weights, earlier, total, pad, shifted = refs
    rows = blocks[0].shape[0]
    flip = place[2]

    def body(sums):
        halo_terms(place, blocks, [place[h] for h in halves], weights, pad, shifted, sums)
        for m in range(rows):
            i = m + flip * (rows - 1 - 2 * m)
            total[i] = earlier[i] + collect(sums, m)

    with_sums(rows, body)


def last_kernel(halves, place, *refs):
    *blocks, weights, earlier, source, image, pad, shifted = refs
    rows = blocks[0].shape[0]
    flip = place[2]

    def body(sums):
        halo_terms(place, blocks, [place[h] for h in halves], weights, pad, shifted, sums)
        for m in range(rows):
            i = m + flip * (rows - 1 - 2 * m)
            coupled = (earlier[i] + collect(sums, m)).T
            image[i] = (source[i].astype(jnp.float32) - coupled).astype(jnp.bfloat16)

    with_sums(rows, body)


def run(body, name, place, operands, blocks, rows, shape, dtype, tiles):
    vmem = pl.BlockSpec(memory_space=pltpu.VMEM)
    return pl.pallas_call(
        body,
        out_shape=jax.ShapeDtypeStruct(shape, dtype),
        in_specs=[pl.BlockSpec(memory_space=pltpu.SMEM)] + [vmem] * len(operands),
        out_specs=vmem,
        scratch_shapes=[
            pltpu.VMEM((rows, MXU // LANES, LANES + 2 * EDGE, LANES), jnp.float32),
            pltpu.VMEM((blocks, OFF, rows, LANES, MXU), jnp.bfloat16),
        ],
        compiler_params=pltpu.CompilerParams(vmem_limit_bytes=16 << 20),
        cost_estimate=pl.CostEstimate(
            flops=2 * tiles * LANES * MXU * MXU, bytes_accessed=0, transcendentals=0
        ),
        name=name,
    )(place, *operands)


def paired(source, kernel):
    devices = lax.axis_size("space")
    here, half = lax.axis_index("space"), lax.axis_index("chan")
    own = jnp.transpose(source, (1, 0, 2))
    rows = own.shape[0]
    swap = [(0, 1), (1, 0)]
    near = [(i, i ^ 1) for i in range(devices) if i ^ 1 < devices]
    far = [(i, ((i + 1) ^ 1) - 1) for i in range(devices)]
    far = [(i, j) for i, j in far if 0 <= j < devices]
    even = (1 - here % 2).astype(jnp.int32)
    place_near = jnp.stack([half, 1 - half, even]).astype(jnp.int32)
    place_far = jnp.stack([half, 1 - half, 1 - even]).astype(jnp.int32)

    other = lax.ppermute(own, "chan", swap)
    near_own = lax.ppermute(own, "space", near)
    far_own = lax.ppermute(own, "space", far)
    near_other = lax.ppermute(near_own, "chan", swap)
    far_other = lax.ppermute(far_own, "chan", swap)

    steps = 2 * OFF * sum(range(rows + 1))
    sums = (rows, LANES, MXU)
    total = run(
        own_kernel, "own", place_near, [own, other, kernel], 2, rows, sums, jnp.float32,
        2 * OFF * rows * rows,
    )
    total = run(
        functools.partial(halo_kernel, (0, 1)), "near", place_near,
        [near_own, near_other, kernel, total], 2, rows, sums, jnp.float32, steps,
    )
    total = run(
        functools.partial(halo_kernel, (0,)), "far_own", place_far,
        [far_own, kernel, total], 1, rows, sums, jnp.float32, steps // 2,
    )
    image = run(
        functools.partial(last_kernel, (1,)), "far_other", place_far,
        [far_other, kernel, total, own], 1, rows, own.shape, jnp.bfloat16, steps // 2,
    )
    return jnp.transpose(image, (1, 0, 2))


def shards(source, kernel):
    channels, rows, columns = source.shape
    fits = channels == MXU and columns == LANES and rows == REACH
    if lax.axis_size("chan") == 2 and fits and kernel.shape[2] == MXU:
        return paired(source, kernel)
    return general(source, kernel)


def solution(mesh):
    placed = (P("chan", "space", None), P(None, None, "chan", None))
    return jax.shard_map(
        shards, mesh=mesh, in_specs=placed, out_specs=P("chan", "space", None), check_vma=False
    )
```

```python
import functools

import jax
import jax.numpy as jnp
from jax import lax
from jax.experimental import pallas as pl
from jax.experimental.pallas import tpu as pltpu
from jax.sharding import PartitionSpec as P

OFF = 7
REACH = (OFF - 1) // 2
MXU = 256
LANES = 128
EDGE = 8
UNITS = 2
FIRST = 2 * 10**9
SECOND = 2 * 10**9


def padded_2(array, sides, width):
    for axis, dim in sides:
        devices, length = (lax.axis_size(axis), array.shape[dim])
        up = [(i, (i + 1) % devices) for i in range(devices - 1)]
        down = [(j, i) for i, j in up]
        last = lax.slice_in_dim(array, length - width, length, axis=dim)
        initial = lax.slice_in_dim(array, 0, width, axis=dim)
        before = lax.ppermute(last, axis, up)
        after = lax.ppermute(initial, axis, down)
        array = jnp.concatenate([before, array, after], axis=dim)
    return array


def correlate(kernel, padded, height):
    width_cols = padded.shape[2]
    widened = jnp.pad(padded, ((0, 0), (0, 0), (REACH, REACH)))
    total = jnp.zeros((kernel.shape[2], height, width_cols), jnp.float32)
    for row_shift in range(OFF):
        window = widened[:, row_shift : row_shift + height, :]
        stacked = jnp.stack(
            [window[:, :, col_shift : col_shift + width_cols] for col_shift in range(OFF)]
        )
        weights = kernel[row_shift]
        total = total + jnp.einsum(
            "boc,bcxy->oxy", weights, stacked, preferred_element_type=jnp.float32
        )
    return total


def general(source, kernel):
    height = source.shape[1]
    gathered = lax.all_gather(source, "chan", axis=0, tiled=True)
    rimmed = padded_2(gathered, (("space", 1),), REACH)
    coupled = correlate(kernel, rimmed, height)
    return (source.astype(jnp.float32) - coupled).astype(jnp.bfloat16)


def spread(block, row_of, pad, shifted):
    rows = block.shape[0]
    for q in range(rows):
        turned = block[row_of(q)].astype(jnp.float32).T
        for part in range(MXU // LANES):
            lanes = slice(part * LANES, (part + 1) * LANES)
            pad[q, part, pl.ds(EDGE, LANES), :] = turned[:, lanes]
            for b in range(OFF):
                view = pad[q, part, pl.ds(EDGE + b - REACH, LANES), :]
                shifted[b, q, :, lanes] = view.astype(jnp.bfloat16)


def clear_edges(pad):
    rows, parts = pad.shape[:2]
    blank = jnp.zeros((EDGE, LANES), jnp.float32)
    for q in range(rows):
        for part in range(parts):
            pad[q, part, pl.ds(0, EDGE), :] = blank
            pad[q, part, pl.ds(EDGE + LANES, EDGE), :] = blank


def multiply(tiles, weights, shifted, sums):
    rows = len(sums) // UNITS
    load, stage = [0] * UNITS, [0] * UNITS
    for n, a, half, b, pairs in tiles:
        unit = load.index(min(load))
        load[unit] += max(len(pairs), 2)
        slot = stage[unit]
        stage[unit] ^= 1
        lanes = pl.ds(pl.multiple_of(half * MXU, MXU), MXU)
        pltpu.matmul_push_rhs(
            weights[a, b, :, lanes], staging_register=slot, mxu_index=unit, transpose=True
        )
        for order, (q, i) in enumerate(pairs):
            pltpu.matmul_acc_lhs(
                sums[unit * rows + i],
                shifted[n, b, q],
                load_staged_rhs=slot if order == 0 else None,
            )


def collect(sums, i):
    rows = len(sums) // UNITS
    value = pltpu.matmul_pop(sums[i])
    for unit in range(1, UNITS):
        value = value + pltpu.matmul_pop(sums[unit * rows + i])
    return value


def with_sums(rows, body):
    refs = [
        pltpu.ACC(unit)((LANES, MXU), jnp.float32) for unit in range(UNITS) for _ in range(rows)
    ]
    pl.run_scoped(lambda *sums: body(sums), *refs)


def place_of(side):
    half = lax.axis_index("chan")
    odd = lax.axis_index("space") % 2
    return half, 1 - half, odd if side == "far" else 1 - odd


def own_kernel(*refs):
    place = place_of("own")
    *blocks, weights, total, pad, shifted = refs
    rows = blocks[0].shape[0]

    def body(sums):
        clear_edges(pad)
        tiles = []
        for n, block in enumerate(blocks):
            spread(block, lambda q: q, pad, shifted.at[n])
            half = place[n]
            for b in range(OFF):
                for a in range(OFF):
                    pairs = [(q, q - a + REACH) for q in range(rows)]
                    pairs = [(q, i) for q, i in pairs if 0 <= i < rows]
                    if pairs:
                        tiles.append((n, a, half, b, pairs))
        multiply(tiles, weights, shifted, sums)
        for i in range(rows):
            total[i] = collect(sums, i)

    with_sums(rows, body)


def halo_terms(place, blocks, halves, weights, pad, shifted, sums):
    rows = blocks[0].shape[0]
    flip = place[2]
    clear_edges(pad)
    tiles = []
    for n, block in enumerate(blocks):
        spread(block, lambda q: q + flip * (rows - 1 - 2 * q), pad, shifted.at[n])
        for b in range(OFF):
            for t in range(rows):
                a = t + flip * (OFF - 1 - 2 * t)
                tiles.append((n, a, halves[n], b, [(m + t, m) for m in range(rows - t)]))
    multiply(tiles, weights, shifted, sums)


def halo_kernel(side, halves, *refs):
    place = place_of(side)
    *blocks, weights, earlier, total, pad, shifted = refs
    rows = blocks[0].shape[0]
    flip = place[2]

    def body(sums):
        halo_terms(place, blocks, [place[h] for h in halves], weights, pad, shifted, sums)
        for m in range(rows):
            i = m + flip * (rows - 1 - 2 * m)
            total[i] = earlier[i] + collect(sums, m)

    with_sums(rows, body)


def last_kernel(side, halves, *refs):
    place = place_of(side)
    *blocks, weights, earlier, source, image, pad, shifted = refs
    rows = blocks[0].shape[0]
    flip = place[2]

    def body(sums):
        halo_terms(place, blocks, [place[h] for h in halves], weights, pad, shifted, sums)
        for m in range(rows):
            i = m + flip * (rows - 1 - 2 * m)
            coupled = (earlier[i] + collect(sums, m)).T
            image[i] = (source[i].astype(jnp.float32) - coupled).astype(jnp.bfloat16)

    with_sums(rows, body)


def run(body, operands, blocks, rows, shape, dtype, tiles):
    vmem = pl.BlockSpec(memory_space=pltpu.VMEM)
    return pl.pallas_call(
        body,
        out_shape=jax.ShapeDtypeStruct(shape, dtype),
        in_specs=[vmem] * len(operands),
        out_specs=vmem,
        scratch_shapes=[
            pltpu.VMEM((rows, MXU // LANES, LANES + 2 * EDGE, LANES), jnp.float32),
            pltpu.VMEM((blocks, OFF, rows, LANES, MXU), jnp.bfloat16),
        ],
        compiler_params=pltpu.CompilerParams(vmem_limit_bytes=16 << 20),
        cost_estimate=pl.CostEstimate(
            flops=2 * tiles * LANES * MXU * MXU, bytes_accessed=0, transcendentals=0
        ),
    )(*operands)


def opening(cost):
    def body(out):
        del out

    return pl.pallas_call(
        body,
        out_shape=jax.ShapeDtypeStruct((EDGE, LANES), jnp.float32),
        out_specs=pl.BlockSpec(memory_space=pl.ANY),
        compiler_params=pltpu.CompilerParams(vmem_limit_bytes=1 << 20, has_side_effects=True),
        cost_estimate=pl.CostEstimate(flops=cost, bytes_accessed=0, transcendentals=0),
    )()


def paired(source, kernel):
    devices = lax.axis_size("space")
    first = opening(FIRST)
    source, first = lax.optimization_barrier((source, first))
    own = jnp.transpose(source, (1, 0, 2))
    rows = own.shape[0]
    swap = [(0, 1), (1, 0)]
    near = [(i, i ^ 1) for i in range(devices) if i ^ 1 < devices]
    far = [(i, ((i + 1) ^ 1) - 1) for i in range(devices)]
    far = [(i, j) for i, j in far if 0 <= j < devices]

    other = lax.ppermute(own, "chan", swap)
    near_own = lax.ppermute(own, "space", near)
    far_own = lax.ppermute(own, "space", far)
    second = opening(SECOND)
    own, second = lax.optimization_barrier((own, second))

    steps = 2 * OFF * sum(range(rows + 1))
    sums = (rows, LANES, MXU)
    total = run(
        own_kernel, [own, other, kernel], 2, rows, sums, jnp.float32,
        2 * OFF * rows * rows,
    )
    near_other = lax.ppermute(near_own, "chan", swap)
    total = run(
        functools.partial(halo_kernel, "near", (0,)),
        [near_own, kernel, total], 1, rows, sums, jnp.float32, steps // 2,
    )
    total = run(
        functools.partial(halo_kernel, "near", (1,)),
        [near_other, kernel, total], 1, rows, sums, jnp.float32, steps // 2,
    )
    far_other = lax.ppermute(far_own, "chan", swap)
    total = run(
        functools.partial(halo_kernel, "far", (0,)),
        [far_own, kernel, total], 1, rows, sums, jnp.float32, steps // 2,
    )
    image = run(
        functools.partial(last_kernel, "far", (1,)),
        [far_other, kernel, total, own], 1, rows, own.shape, jnp.bfloat16, steps // 2,
    )
    return jnp.transpose(image, (1, 0, 2))


def shards(source, kernel):
    channels, rows, columns = source.shape
    fits = channels == MXU and columns == LANES and rows == REACH
    if lax.axis_size("chan") == 2 and fits and kernel.shape[2] == MXU:
        return paired(source, kernel)
    return general(source, kernel)


def solution(mesh):
    placed = (P("chan", "space", None), P(None, None, "chan", None))
    return jax.shard_map(
        shards, mesh=mesh, in_specs=placed, out_specs=P("chan", "space", None), check_vma=False
    )
```
